256 devices in a mesh: grp: 32 (over x, z_lo, core), tp: 8 (over z_hi, y).
Axes of the slice: x: 4, y: 4, z: 8 (z_hi: 2, z_lo: 4; z = z_hi * 4 + z_lo), core: 2. Of those that a mesh axis runs over, the one named last changes fastest.
Arguments:
- kv_weight: bfloat16 [8192, 2048], P('tp'), may hold values from -0.0625 to 0.0625
- kv_bias: bfloat16 [2048], P('tp'), may hold values from -3 to 3
- hidden_in: bfloat16 [4, 32, 48, 8192], P(None, 'grp', None, 'tp'), may hold values from -6 to 6
- queries: bfloat16 [4, 32, 48, 8192], P(None, 'grp', None, 'tp'), may hold values from -139 to 139
- res_cache: bfloat16 [32, 16, 128, 2048], P('grp', None, None, 'tp'), may hold values from -6 to 6
- res_len: int32 [32, 16], P('grp'), may hold values from 1 to 128, 1088 in all within a row
- long_cache: bfloat16 [32, 32, 512, 2048], P('grp', None, None, 'tp'), may hold values from -6 to 6
- long_len: int32 [32, 32], replicated, may hold values from 1 to 512, 8192 in all within a row
- long_dest: int32 [32, 32], replicated, may hold values from 0 to 31, each once within a row
Outputs:
- attention_out: bfloat16 [4, 32, 48, 8192], P(None, 'grp', None, 'tp')
The draws below stay inside these ranges and needn't reach their ends.
Inputs may be any that keep to these rules, and one draw needn't show every extreme that they name: `res_len`: each group's lengths sum to 1088, and the largest is 128. `long_len`: each home group's lengths sum to 8192, and the largest is 512. `long_dest`: each row is a permutation of the groups, so every group sends one request to every group and receives one from every group.
All inputs are finite; a program needn't handle non-finite values.
Results may differ from the reference program's by a relative error of at most 0.0051.
Values may be sent and summed in bfloat16 or wider, within the bound.
A program may use at most 128 MiB of HBM per device.

```python
import math
import jax
import jax.numpy as jnp
import numpy as np
from jax import lax

D = 8192
H = 64
KVH = 8
HS = 128
STEPS = 4
RES = 16
SHORT = 128
LONG = 512
GROUPS = 32
RQ = 48
N_GRP = 32


def draw_queries(key, part):
    rows = RES + GROUPS
    shape = (STEPS, GROUPS, rows, H * HS)
    values = jnp.clip(jax.random.normal(key, shape, jnp.float32), -6.0, 6.0)
    return values.astype(jnp.bfloat16)


def level_of(key, extent, cuts, low, top_value):
    def one(dim, parts):
        steps = jax.random.uniform(jax.random.fold_in(jax.random.fold_in(key, 6), dim), (parts,), jnp.float32, low / len(cuts), top_value / len(cuts))
        return jnp.repeat(jnp.exp(steps), extent[dim] // parts).reshape((-1,) + (1,) * (len(extent) - dim - 1))

    loudness = one(*cuts[0])
    for cut in cuts[1:]:
        loudness = loudness * one(*cut)
    return loudness


def split_up(count, total, bound, lean):
    weights = [(1 << 20) // math.isqrt(rank ** lean) + 1 for rank in range(2, count + 1)]
    surplus, given = total - bound - (count - 1), [1] * (count - 1)
    while surplus > 0:
        movable = [i for i in range(count - 1) if given[i] < bound]
        pool, budget = sum([weights[i] for i in movable]), surplus
        for i in movable:
            addition = min(bound - given[i], max(1, budget * weights[i] // pool), surplus)
            given[i] = given[i] + addition
            surplus = surplus - addition
    return np.array([bound] + given)


def ragged_sizes(stream_key, number_of, total, most, skew):
    if number_of == 2:
        one = jax.random.randint(stream_key, (), max(1, total - most), min(most, total - 1) + 1)
        return jnp.stack([one, total - one])
    tallies = jnp.asarray(split_up(number_of, total, most, skew), jnp.int32)
    pairs = (number_of - 1) // 2
    giver, sink = tallies[1:1 + 2 * pairs:2], tallies[2:2 + 2 * pairs:2]
    slack = jnp.minimum(giver - 1, most - sink)
    moved = jax.random.randint(jax.random.fold_in(stream_key, 1), (pairs,), 0, 1 << 20) % (slack + 1)
    tallies = tallies.at[1:1 + 2 * pairs:2].set(giver - moved).at[2:2 + 2 * pairs:2].set(sink + moved)
    return tallies[jax.random.permutation(jax.random.fold_in(stream_key, 2), number_of)]


def noise(own_key, dims, width, reach, shards=(), kind=jnp.bfloat16):
    entries = jax.random.normal(own_key, dims, jnp.float32) * width
    if len(shards) > 0:
        entries = level_of(own_key, dims, shards, -0.22, 0.18) * entries
    return jnp.clip(entries, min=-reach, max=reach).astype(kind)


def setup_inputs(seed: int = 0) -> dict:
    arg_keys = jax.random.split(jax.random.key(seed), 10)
    kv_weight = noise(arg_keys[0], (D, 2 * KVH * HS), D ** -0.5, 0.0625, ((0, 8),))
    kv_bias = noise(arg_keys[1], (2 * KVH * HS,), 0.5, 3.0, ((0, 8),))
    hidden_in = noise(arg_keys[2], (STEPS, GROUPS, RQ, D), 1.0, 6.0, ((1, 32), (3, 8)))
    queries = draw_queries(jax.random.fold_in(arg_keys[9], 71), 0)
    res_cache = noise(arg_keys[4], (GROUPS, RES, SHORT, 2 * KVH * HS), 1.0, 6.0, ((0, 32), (3, 8)))
    res_len = jax.vmap(lambda own: ragged_sizes(own, RES, (RES + 1) * SHORT // 2, SHORT, 2))(jax.random.split(arg_keys[5], GROUPS)).reshape((GROUPS, RES)).astype(jnp.int32)
    long_cache = noise(arg_keys[6], (GROUPS, GROUPS, LONG, 2 * KVH * HS), 1.0, 6.0, ((0, 32), (3, 8)))
    long_len = jax.vmap(lambda own: ragged_sizes(own, GROUPS, GROUPS * LONG // 2, LONG, 2))(jax.random.split(arg_keys[7], GROUPS)).reshape((GROUPS, GROUPS)).astype(jnp.int32)
    long_dest = jax.vmap(lambda own: jax.random.permutation(own, GROUPS))(jax.random.split(arg_keys[8], GROUPS)).reshape((GROUPS, GROUPS)).astype(jnp.int32)
    return dict(kv_weight=kv_weight, kv_bias=kv_bias, hidden_in=hidden_in, queries=queries, res_cache=res_cache, res_len=res_len, long_cache=long_cache, long_len=long_len, long_dest=long_dest)


ROPE_BASE = 1000000.0
masked_score = -1.0e30


def rotate(keys_raw, positions):
    half_dim = HS // 2
    freqs = jnp.power(jnp.float32(ROPE_BASE), -2.0 * jnp.arange(half_dim, dtype=jnp.float32) / HS)
    angles = positions.astype(jnp.float32)[..., None] * freqs
    cosine = jnp.cos(angles)
    sine = jnp.sin(angles)
    first_half = keys_raw[..., :half_dim]
    second_half = keys_raw[..., half_dim:]
    return jnp.concatenate([first_half * cosine - second_half * sine, second_half * cosine + first_half * sine], axis=-1)


def attend(query, cache, lengths, new_keys, new_values):
    kv_heads = new_keys.shape[2]
    capacity = cache.shape[1]
    cache = cache.reshape(cache.shape[0], capacity, kv_heads, 2 * HS).astype(jnp.float32)
    old_keys = cache[..., :HS]
    old_values = cache[..., HS:]
    query = query.astype(jnp.float32)
    scale = HS ** -0.5
    scores_old = jnp.einsum("sbkqd,bckd->sbkqc", query, old_keys) * scale
    valid = jnp.arange(capacity, dtype=jnp.int32)[None, :] < lengths[:, None]
    scores_old = jnp.where(valid[None, :, None, None, :], scores_old, masked_score)
    scores_new = jnp.einsum("sbkqd,tbkd->sbkqt", query, new_keys.astype(jnp.float32)) * scale
    step_count = new_keys.shape[0]
    causal = jnp.arange(step_count)[None, :] <= jnp.arange(step_count)[:, None]
    scores_new = jnp.where(causal[:, None, None, None, :], scores_new, masked_score)
    highest = jnp.maximum(jnp.max(scores_old, -1), jnp.max(scores_new, -1))[..., None]
    probs_old = jnp.exp(scores_old - highest)
    probs_new = jnp.exp(scores_new - highest)
    total = jnp.sum(probs_old, -1, keepdims=True) + jnp.sum(probs_new, -1, keepdims=True)
    weights_old = (probs_old / total).astype(jnp.bfloat16).astype(jnp.float32)
    weights_new = (probs_new / total).astype(jnp.bfloat16).astype(jnp.float32)
    mixed = jnp.einsum("sbkqc,bckd->sbkqd", weights_old, old_values)
    mixed = mixed + jnp.einsum("sbkqt,tbkd->sbkqd", weights_new, new_values.astype(jnp.float32))
    return mixed.astype(jnp.bfloat16)


def reference(kv_weight, kv_bias, hidden_in, queries, res_cache, res_len, long_cache, long_len, long_dest):
    group_count = N_GRP
    serve_rows = RES + group_count
    q_per_kv = H // KVH

    def one_group(group):
        hidden_rows = lax.dynamic_index_in_dim(hidden_in, group, 1, keepdims=False)
        hidden_rows = hidden_rows.reshape(STEPS * serve_rows, D)
        kv_new = jnp.dot(hidden_rows, kv_weight, preferred_element_type=jnp.float32) + kv_bias.astype(jnp.float32)
        kv_new = kv_new.reshape(STEPS, serve_rows, KVH, 2 * HS)
        matched = (long_dest == group).astype(jnp.int32)
        picked = jnp.argmax(matched, axis=1).astype(jnp.int32)
        len_in = jnp.sum(matched * long_len, axis=1).astype(jnp.int32)
        arrived = long_cache[jnp.arange(group_count, dtype=jnp.int32), picked]
        own_len = lax.dynamic_index_in_dim(res_len, group, 0, keepdims=False).astype(jnp.int32)
        own_cache = lax.dynamic_index_in_dim(res_cache, group, 0, keepdims=False)
        served_len = jnp.concatenate([own_len, len_in])
        positions = served_len[None, :] + jnp.arange(STEPS, dtype=jnp.int32)[:, None]
        new_keys = rotate(kv_new[..., :HS], positions[:, :, None]).astype(jnp.bfloat16)
        new_values = kv_new[..., HS:].astype(jnp.bfloat16)
        query = lax.dynamic_index_in_dim(queries, group, 1, keepdims=False)
        query = query.reshape(STEPS, serve_rows, KVH, q_per_kv, HS)
        staying = attend(query[:, :RES], own_cache, own_len, new_keys[:, :RES], new_values[:, :RES])
        moving = attend(query[:, RES:], arrived, len_in, new_keys[:, RES:], new_values[:, RES:])
        joined = jnp.concatenate([staying, moving], axis=1)
        return joined.reshape(STEPS, serve_rows, H * HS)

    results = lax.map(one_group, jnp.arange(group_count, dtype=jnp.int32))
    return jnp.transpose(results, (1, 0, 2, 3))
```

```python
import jax
import jax.numpy as jnp
from jax import lax
from jax.sharding import PartitionSpec as P

HS = 128
ROPE_BASE = 1000000.0
masked_score = -1e30


def rotate(keys_raw, positions):
    half_dim = HS // 2
    freqs = jnp.power(jnp.float32(ROPE_BASE), -2.0 * jnp.arange(half_dim, dtype=jnp.float32) / HS)
    angles = positions.astype(jnp.float32)[..., None] * freqs
    cosine = jnp.cos(angles)
    sine = jnp.sin(angles)
    first_half = keys_raw[..., :half_dim]
    second_half = keys_raw[..., half_dim:]
    return jnp.concatenate(
        [first_half * cosine - second_half * sine, second_half * cosine + first_half * sine],
        axis=-1,
    )


def cached(query, cache, lengths):
    keys, values = cache[..., :HS], cache[..., HS:]
    scores = jnp.einsum("brd,bcd->brc", query, keys, preferred_element_type=jnp.float32) * HS**-0.5
    valid = jnp.arange(cache.shape[1], dtype=jnp.int32)[None, :] < lengths[:, None]
    scores = jnp.where(valid[:, None, :], scores, masked_score)
    top = jnp.max(scores, -1, keepdims=True)
    probs = jnp.exp(scores - top)
    total = jnp.sum(probs, -1, keepdims=True)
    mixed = jnp.einsum(
        "brc,bcd->brd", probs.astype(jnp.bfloat16), values, preferred_element_type=jnp.float32
    )
    return mixed / total, top + jnp.log(total)


def per_device(
    kv_weight, kv_bias, hidden_in, queries, res_cache, res_len, long_cache, long_len, long_dest
):
    steps, _, rows, width = hidden_in.shape
    groups = long_dest.shape[0]
    stay = rows - groups
    heads = queries.shape[3] // HS
    group = lax.axis_index("grp")

    part = jnp.dot(
        hidden_in.reshape(steps * rows, width), kv_weight, preferred_element_type=jnp.float32
    )
    kv = lax.psum_scatter(part, "tp", scatter_dimension=1, tiled=True)
    kv = (kv + kv_bias.astype(jnp.float32)).reshape(steps, rows, 2 * HS)

    matched = (long_dest == group).astype(jnp.int32)
    served = jnp.concatenate([res_len[0], jnp.sum(matched * long_len, axis=1)])
    positions = served[None, :] + jnp.arange(steps, dtype=jnp.int32)[:, None]
    new_keys = rotate(kv[..., :HS], positions).astype(jnp.bfloat16)
    new_values = kv[..., HS:].astype(jnp.bfloat16)

    query = queries[:, 0].reshape(steps, rows, heads, HS).transpose(1, 0, 2, 3)
    query = query.reshape(rows, steps * heads, HS)
    came = lax.all_to_all(query[stay:], "grp", split_axis=0, concat_axis=0, tiled=True)
    own_dest = lax.dynamic_index_in_dim(long_dest, group, 0, keepdims=False)
    own_long = lax.dynamic_index_in_dim(long_len, group, 0, keepdims=False)
    out, lse = cached(came[own_dest], long_cache[0], own_long)
    pick = jnp.argsort(own_dest)
    back = lax.all_to_all(out.astype(jnp.bfloat16)[pick], "grp", 0, 0, tiled=True)
    back_lse = lax.all_to_all(lse[pick], "grp", 0, 0, tiled=True)
    out_res, lse_res = cached(query[:stay], res_cache[0], res_len[0])
    old = jnp.concatenate([out_res, back.astype(jnp.float32)])
    old_lse = jnp.concatenate([lse_res, back_lse])

    scores = jnp.einsum("brd,tbd->brt", query, new_keys, preferred_element_type=jnp.float32)
    scores = scores * HS**-0.5
    step_of = jnp.arange(steps * heads, dtype=jnp.int32) // heads
    seen = jnp.arange(steps, dtype=jnp.int32)[None, :] <= step_of[:, None]
    scores = jnp.where(seen[None], scores, masked_score)
    top = jnp.maximum(jnp.max(scores, -1, keepdims=True), old_lse)
    probs = jnp.exp(scores - top)
    share = jnp.exp(old_lse - top)
    total = jnp.sum(probs, -1, keepdims=True) + share
    mixed = jnp.einsum(
        "brt,tbd->brd", (probs / total).astype(jnp.bfloat16), new_values,
        preferred_element_type=jnp.float32,
    )
    mixed = mixed + old * (share / total)
    mixed = mixed.astype(jnp.bfloat16).reshape(rows, steps, heads * HS).transpose(1, 0, 2)
    return mixed[:, None]


def solution(mesh):
    placed = (
        P("tp", None),
        P("tp"),
        P(None, "grp", None, "tp"),
        P(None, "grp", None, "tp"),
        P("grp", None, None, "tp"),
        P("grp", None),
        P("grp", None, None, "tp"),
        P(),
        P(),
    )
    return jax.shard_map(
        per_device,
        mesh=mesh,
        in_specs=placed,
        out_specs=P(None, "grp", None, "tp"),
        check_vma=False,
    )
```
